512 devices in a mesh: head: 32 (over x, z), seq: 16 (over y, core).
Axes of the slice: x: 4, y: 8, z: 8, core: 2. Of those that a mesh axis runs over, the one named last changes fastest.
Arguments:
- queries: bfloat16 [16, 4096, 4096], P('seq', 'head'), may hold values from -8 to 8
- key_row_matrix: bfloat16 [16, 4096, 1024], P('seq', 'head'), may hold values from -8 to 8
- values: bfloat16 [16, 4096, 1024], P('seq', 'head'), may hold values from -6 to 6
- verticals: int32 [32, 6], replicated, may hold values from 0 to 511, as said below
- slashes: int32 [32, 3], replicated, may hold values from 1 to 31, as said below
- counts: int32 [32, 2], replicated, may hold values from 0 to 6, as said below
Outputs:
- context: bfloat16 [16, 4096, 4096], P('seq', 'head')
The draws below stay inside these ranges and needn't reach their ends.
Inputs may be any that keep to these rules, and one draw needn't show every extreme that they name: `verticals`: each row holds 6 different key blocks. `slashes`: each row holds 3 different block offsets. `counts`: column 0 is at least 1; some head uses all 6 and all 3 slots.
All inputs are finite; a program needn't handle non-finite values.
Results may differ from the reference program's by a relative error of at most 0.0037.
Values may be sent and summed in bfloat16 or wider, within the bound.
No kernel may reach another device: no remote copies, remote signals or barrier semaphores. Data moves between devices by JAX's collectives and lax.ppermute only.
A program may use at most 64 MiB of HBM per device.

```python
import math
import jax
import jax.numpy as jnp
from jax import lax

QUERY_HEADS = 32
KEY_VALUE_HEADS = 8
HEAD_WIDTH = 128
BLOCK_TOKENS = 128
NV = 6
NS = 3
SEGMENT_TOKENS = 4096
SEGBLK = 32
SEGMENT_COUNT = 16
BLOCK_COUNT = 512


def draw_queries(key, part):
    array_shape = (SEGMENT_COUNT, SEGMENT_TOKENS, QUERY_HEADS * HEAD_WIDTH)
    drawn = jax.random.truncated_normal(jax.random.fold_in(key, 11), -6.0, 6.0, array_shape)
    return drawn.astype(jnp.bfloat16)


def draw_key_row_matrix(key, part):
    array_shape = (SEGMENT_COUNT, SEGMENT_TOKENS, KEY_VALUE_HEADS * HEAD_WIDTH)
    drawn = jax.random.truncated_normal(jax.random.fold_in(key, 13), -6.0, 6.0, array_shape)
    return drawn.astype(jnp.bfloat16)


def draw_verticals(key, part):
    head_keys = jax.random.split(jax.random.fold_in(key, 21), QUERY_HEADS)
    picked = jax.vmap(lambda item: jax.random.permutation(item, BLOCK_COUNT)[:NV])(head_keys)
    return picked.astype(jnp.int32)


def draw_slashes(key, part):
    head_keys = jax.random.split(jax.random.fold_in(key, 31), QUERY_HEADS)
    picked = jax.vmap(lambda item: jax.random.permutation(item, SEGBLK - 1)[:NS] + 1)(head_keys)
    widest = jnp.concatenate([jax.random.permutation(jax.random.fold_in(key, 32), SEGBLK - 2)[:NS - 1] + 1, jnp.array([SEGBLK - 1], dtype=jnp.int32)])
    chosen = jax.random.randint(jax.random.fold_in(key, 33), (), 0, QUERY_HEADS)
    picked = picked.at[chosen].set(widest.astype(picked.dtype))
    return picked.astype(jnp.int32)


def draw_counts(key, part):
    dense = jax.random.randint(jax.random.fold_in(key, 41), (QUERY_HEADS,), 0, 4) == 0
    light_columns = jax.random.randint(jax.random.fold_in(key, 42), (QUERY_HEADS,), 1, 3)
    light_slashes = jax.random.randint(jax.random.fold_in(key, 43), (QUERY_HEADS,), 0, 2)
    fullest = jax.random.randint(jax.random.fold_in(key, 44), (), 0, QUERY_HEADS)
    sparsest = (fullest + jax.random.randint(jax.random.fold_in(key, 45), (), 1, QUERY_HEADS)) % QUERY_HEADS
    column_use = jnp.where(dense, NV, light_columns)
    slash_use = jnp.where(dense, NS, light_slashes)
    column_use = column_use.at[fullest].set(NV).at[sparsest].set(1)
    slash_use = slash_use.at[fullest].set(NS).at[sparsest].set(0)
    return jnp.stack([column_use, slash_use], axis=1).astype(jnp.int32)


def level_of(stream_key, dims, cuts, smallest, largest):
    gain, own = 1.0, jax.random.fold_in(stream_key, 6)
    for axis_at, shards_of in cuts:
        heights = jnp.exp(jax.random.uniform(jax.random.fold_in(own, axis_at), (shards_of,), jnp.float32, smallest / len(cuts), largest / len(cuts)))
        gain = gain * jnp.repeat(heights, dims[axis_at] // shards_of).reshape([-1 if axis == axis_at else 1 for axis in range(len(dims))])
    return gain


def scatter_about(stream_key, dims, width, bound, cuts=(), held_as=jnp.bfloat16):
    result = width * jax.random.normal(stream_key, dims, jnp.float32)
    if cuts:
        result = result * level_of(stream_key, dims, cuts, -0.22, 0.18)
    return jnp.clip(result, -bound, bound).astype(held_as)


def setup_inputs(seed: int = 0) -> dict:
    seeds = jax.random.split(jax.random.key(seed), 7)
    return {
        "queries": draw_queries(jax.random.fold_in(seeds[6], 71), 0),
        "key_row_matrix": draw_key_row_matrix(jax.random.fold_in(seeds[6], 71), 0),
        "values": scatter_about(seeds[2], (SEGMENT_COUNT, SEGMENT_TOKENS, KEY_VALUE_HEADS * HEAD_WIDTH), 1.0, 6.0, ((0, 16), (1, 32))),
        "verticals": draw_verticals(jax.random.fold_in(seeds[6], 71), 0),
        "slashes": draw_slashes(jax.random.fold_in(seeds[6], 71), 0),
        "counts": draw_counts(jax.random.fold_in(seeds[6], 71), 0),
    }


def head_attention(query, key_block, value_block, columns, offsets, in_use):
    group_ids = jnp.arange(SEGBLK, dtype=jnp.int32)
    row_ids = jnp.arange(BLOCK_TOKENS, dtype=jnp.int32)
    causal = row_ids[:, None] >= row_ids[None, :]
    slash_live = jnp.arange(NS, dtype=jnp.int32) < in_use[1]
    column_live = jnp.arange(NV, dtype=jnp.int32) < in_use[0]
    later_slot = jnp.arange(1 + NS + NV, dtype=jnp.int32) > 0
    scaling = 1.0 / math.sqrt(HEAD_WIDTH)

    def segment(seg_id):
        block_ids = seg_id * SEGBLK + group_ids
        slash_ids = block_ids[:, None] - offsets[None, :]
        slash_ok = slash_live[None, :] & (slash_ids >= 0)
        repeated = jnp.any(slash_live[None, None, :] & (block_ids[:, None, None] - columns[None, :, None] == offsets[None, None, :]), axis=2)
        column_ok = column_live[None, :] & (columns[None, :] < block_ids[:, None]) & jnp.logical_not(repeated)
        column_ids = jnp.broadcast_to(columns[None, :], (SEGBLK, NV))
        chosen = jnp.concatenate([block_ids[:, None], slash_ids, column_ids], axis=1)
        allowed = jnp.concatenate([jnp.ones((SEGBLK, 1), dtype=bool), slash_ok, column_ok], axis=1)
        chosen = jnp.clip(chosen, 0, BLOCK_COUNT - 1).astype(jnp.int32)
        key_take = key_block[chosen].astype(jnp.float32)
        value_take = value_block[chosen].astype(jnp.float32)
        query_here = lax.dynamic_slice_in_dim(query, seg_id * SEGBLK, SEGBLK, 0).astype(jnp.float32)
        scores = jnp.einsum('gqd,gskd->gqsk', query_here, key_take) * scaling
        visible = allowed[:, None, :, None] & (later_slot[None, None, :, None] | causal[None, :, None, :])
        scores = jnp.where(visible, scores, -jnp.inf)
        row_top = lax.optimization_barrier(jnp.max(scores, axis=(2, 3), keepdims=True))
        weights = jnp.exp(scores - row_top)
        totals = lax.optimization_barrier(jnp.sum(weights, axis=(2, 3)))
        rounded = lax.optimization_barrier(weights.astype(jnp.bfloat16)).astype(jnp.float32)
        mixed = jnp.einsum('gqsk,gskd->gqd', rounded, value_take)
        return (mixed / totals[:, :, None]).astype(jnp.bfloat16)
    return lax.map(segment, jnp.arange(SEGMENT_COUNT, dtype=jnp.int32))

def reference(queries, key_row_matrix, values, verticals, slashes, counts):
    query_all = queries.reshape(BLOCK_COUNT, BLOCK_TOKENS, QUERY_HEADS, HEAD_WIDTH)
    key_complete = key_row_matrix.reshape(BLOCK_COUNT, BLOCK_TOKENS, KEY_VALUE_HEADS, HEAD_WIDTH)
    value_complete = values.reshape(BLOCK_COUNT, BLOCK_TOKENS, KEY_VALUE_HEADS, HEAD_WIDTH)
    group_width = QUERY_HEADS // KEY_VALUE_HEADS

    def one_head(head_id):
        shared = head_id // group_width
        query = lax.dynamic_index_in_dim(query_all, head_id, 2, keepdims=False)
        key_block = lax.dynamic_index_in_dim(key_complete, shared, 2, keepdims=False)
        value_block = lax.dynamic_index_in_dim(value_complete, shared, 2, keepdims=False)
        return head_attention(query, key_block, value_block, verticals[head_id], slashes[head_id], counts[head_id])
    outputs = lax.map(one_head, jnp.arange(QUERY_HEADS, dtype=jnp.int32))
    outputs = jnp.transpose(outputs, (1, 2, 3, 0, 4))
    return outputs.reshape(SEGMENT_COUNT, SEGMENT_TOKENS, QUERY_HEADS * HEAD_WIDTH)
```

```python
import math

import jax
import jax.numpy as jnp
from jax import lax
from jax.experimental import pallas as pl
from jax.experimental.pallas import tpu as pltpu
from jax.sharding import Mesh
from jax.sharding import PartitionSpec as P

QUERY_HEADS = 32
KEY_VALUE_HEADS = 8
HEAD_WIDTH = 128
BLOCK_TOKENS = 128
X_CHIPS = 4
Z_CHIPS = 8
SEGMENTS = 16
NV = 6
NS = 3
SLOTS = 1 + NS + NV
ROW_BLOCKS = 8
SEG_BLOCKS = 32
COLUMN_BASE = 2 * SEG_BLOCKS
POOL_BLOCKS = COLUMN_BASE + NV
GROUP = 4


def shifted(value, axis, distance, size, wrap):
    pairs = [(i, (i + distance) % size) for i in range(size) if wrap or i + distance < size]
    return lax.ppermute(value, axis, pairs)


def column_kernel(place_ref, row0, row1, row2, row3, out_ref, sems):
    out_ref[...] = jnp.zeros_like(out_ref)
    rows = (row0, row1, row2, row3)
    for slot in range(NV):
        place = place_ref[slot]
        for which in range(X_CHIPS):
            low = which * ROW_BLOCKS

            @pl.when((place >= low) & (place < low + ROW_BLOCKS))
            def _():
                copy = pltpu.make_async_copy(
                    rows[which].at[place - low], out_ref.at[slot], sems.at[slot]
                )
                copy.start()
                copy.wait()


def own_columns(place, rows):
    return pl.pallas_call(
        column_kernel,
        out_shape=jax.ShapeDtypeStruct((NV, 2, BLOCK_TOKENS, HEAD_WIDTH), jnp.bfloat16),
        grid_spec=pltpu.PrefetchScalarGridSpec(
            num_scalar_prefetch=1,
            grid=(1,),
            in_specs=[pl.BlockSpec(memory_space=pl.ANY)] * X_CHIPS,
            out_specs=pl.BlockSpec(
                (NV, 2, BLOCK_TOKENS, HEAD_WIDTH), lambda i, place_ref: (0, 0, 0, 0)
            ),
            scratch_shapes=[pltpu.SemaphoreType.DMA((NV,))],
        ),
        name="own_columns",
    )(place, *rows)


def attention_kernel(
    index_ref, bias_ref, pairs_ref, query_ref, *rest
):
    rows = rest[:8]
    columns, out_ref, pool, score_ref, top_ref, total_ref, mix_ref, sems = rest[8:]
    copies = [
        pltpu.make_async_copy(
            row, pool.at[pl.ds(at * ROW_BLOCKS, ROW_BLOCKS)], sems.at[at]
        )
        for at, row in enumerate(rows)
    ]
    copies.append(
        pltpu.make_async_copy(columns, pool.at[pl.ds(COLUMN_BASE, NV)], sems.at[8])
    )
    for copy in copies:
        copy.start()
    for copy in copies:
        copy.wait()
    scale = math.log2(math.e) / math.sqrt(HEAD_WIDTH)
    pairs = pairs_ref[0]
    row_ids = lax.broadcasted_iota(jnp.int32, (BLOCK_TOKENS, BLOCK_TOKENS), 0)
    col_ids = lax.broadcasted_iota(jnp.int32, (BLOCK_TOKENS, BLOCK_TOKENS), 1)
    causal_bias = jnp.where(row_ids >= col_ids, 0.0, -jnp.inf)

    def keys_of(slot, block, part):
        return pool[index_ref[slot, block], part]

    def score(pair, group, first):
        for at in range(GROUP):
            block = group * GROUP + at
            key_pair = jnp.concatenate(
                [keys_of(2 * pair, block, 0), keys_of(2 * pair + 1, block, 0)], axis=0
            )
            found = lax.dot_general(
                query_ref[block],
                key_pair,
                (((1,), (1,)), ((), ())),
                preferred_element_type=jnp.float32,
            )
            left = found[:, :BLOCK_TOKENS]
            right = found[:, BLOCK_TOKENS:] + bias_ref[2 * pair + 1, block]
            if first:
                left = left + causal_bias
                top_ref[at] = jnp.maximum(left, right)
            else:
                left = left + bias_ref[2 * pair, block]
                top_ref[at] = jnp.maximum(top_ref[at], jnp.maximum(left, right))
            score_ref[pair, at, :, :BLOCK_TOKENS] = left
            score_ref[pair, at, :, BLOCK_TOKENS:] = right

    def mix(pair, group, first):
        for at in range(GROUP):
            block = group * GROUP + at
            value_pair = jnp.concatenate(
                [keys_of(2 * pair, block, 1), keys_of(2 * pair + 1, block, 1)], axis=0
            )
            top = top_ref[at]
            top = jnp.concatenate([top, top], axis=1)
            weights = jnp.exp2((score_ref[pair, at] - top) * scale)
            total = weights[:, :BLOCK_TOKENS] + weights[:, BLOCK_TOKENS:]
            mixed = jnp.dot(
                weights.astype(jnp.bfloat16), value_pair, preferred_element_type=jnp.float32
            )
            if first:
                total_ref[at] = total
                mix_ref[at] = mixed
            else:
                total_ref[at] += total
                mix_ref[at] += mixed

    def group_step(group, carry):
        score(0, group, True)

        def score_step(pair, inner):
            score(pair, group, False)
            return inner

        lax.fori_loop(1, pairs, score_step, 0)
        for at in range(GROUP):
            top_ref[at] = jnp.broadcast_to(
                jnp.max(top_ref[at], axis=1, keepdims=True), (BLOCK_TOKENS, BLOCK_TOKENS)
            )
        mix(0, group, True)

        def mix_step(pair, inner):
            mix(pair, group, False)
            return inner

        lax.fori_loop(1, pairs, mix_step, 0)
        for at in range(GROUP):
            total = jnp.sum(total_ref[at], axis=1, keepdims=True)
            out_ref[group * GROUP + at] = (mix_ref[at] / total).astype(out_ref.dtype)
        return carry

    lax.fori_loop(0, SEG_BLOCKS // GROUP, group_step, 0)


def attention(index, bias, pairs, query, rows, columns):
    whole = (SEG_BLOCKS, BLOCK_TOKENS, HEAD_WIDTH)
    square = (GROUP, BLOCK_TOKENS, BLOCK_TOKENS)
    return pl.pallas_call(
        attention_kernel,
        out_shape=jax.ShapeDtypeStruct(whole, jnp.bfloat16),
        grid_spec=pltpu.PrefetchScalarGridSpec(
            num_scalar_prefetch=3,
            grid=(1,),
            in_specs=[pl.BlockSpec(whole, lambda i, *refs: (0, 0, 0))]
            + [pl.BlockSpec(memory_space=pl.ANY)] * 9,
            out_specs=pl.BlockSpec(whole, lambda i, *refs: (0, 0, 0)),
            scratch_shapes=[
                pltpu.VMEM((POOL_BLOCKS, 2, BLOCK_TOKENS, HEAD_WIDTH), jnp.bfloat16),
                pltpu.VMEM((SLOTS // 2, GROUP, BLOCK_TOKENS, 2 * BLOCK_TOKENS), jnp.float32),
                pltpu.VMEM(square, jnp.float32),
                pltpu.VMEM(square, jnp.float32),
                pltpu.VMEM(square, jnp.float32),
                pltpu.SemaphoreType.DMA((9,)),
            ],
        ),
        name="attention",
    )(index, bias, pairs, query, *rows, columns)


def slot_tables(columns, offsets, in_use, segment, x_index):
    slots = jnp.arange(SLOTS, dtype=jnp.int32)
    local = jnp.arange(SEG_BLOCKS, dtype=jnp.int32)
    blocks = segment * SEG_BLOCKS + local
    live_slash = jnp.arange(NS, dtype=jnp.int32) < in_use[1]
    slash_hit = slots[:, None] - 1 == jnp.arange(NS, dtype=jnp.int32)[None, :]
    offset = jnp.sum(jnp.where(slash_hit & live_slash[None, :], offsets[None, :], 0), axis=1)
    is_slash = (slots >= 1) & (slots <= in_use[1])
    column_slot = slots - 1 - in_use[1]
    is_column = (column_slot >= 0) & (column_slot < in_use[0])
    column_hit = column_slot[:, None] == jnp.arange(NV, dtype=jnp.int32)[None, :]
    column = jnp.sum(jnp.where(column_hit, columns[None, :], 0), axis=1)
    repeated = jnp.any(
        live_slash[None, None, :]
        & (blocks[None, :, None] - column[:, None, None] == offsets[None, None, :]),
        axis=2,
    )
    column_ok = is_column[:, None] & (column[:, None] < blocks[None, :]) & ~repeated
    slash_ok = is_slash[:, None] & (blocks[None, :] >= offset[:, None])
    source = local[None, :] - offset[:, None] + SEG_BLOCKS
    own = source // SEG_BLOCKS
    inner = source % SEG_BLOCKS
    turn = (x_index - inner // ROW_BLOCKS) % X_CHIPS
    near = own * SEG_BLOCKS + turn * ROW_BLOCKS + inner % ROW_BLOCKS
    far = jnp.clip(COLUMN_BASE + column_slot, COLUMN_BASE, POOL_BLOCKS - 1)
    index = jnp.where(is_column[:, None], far[:, None], near)
    active = (slots == 0)[:, None] | slash_ok | column_ok
    bias = jnp.where(active, 0.0, -jnp.inf).astype(jnp.float32)
    pairs = (in_use[0] + in_use[1] + 2) // 2
    return index.astype(jnp.int32), bias, pairs.astype(jnp.int32).reshape(1)


def shards(queries, key_row_matrix, values, verticals, slashes, counts):
    segment = lax.axis_index("seq")
    x_index = lax.axis_index("x")
    head = lax.axis_index("z") * X_CHIPS + x_index
    columns = lax.dynamic_index_in_dim(verticals, head, 0, keepdims=False)
    offsets = lax.dynamic_index_in_dim(slashes, head, 0, keepdims=False)
    in_use = lax.dynamic_index_in_dim(counts, head, 0, keepdims=False)

    tile = (BLOCK_TOKENS, KEY_VALUE_HEADS, HEAD_WIDTH)
    both = jnp.stack(
        [key_row_matrix.reshape(tile), values.reshape(tile)], axis=0
    ).transpose(2, 0, 1, 3)
    row = lax.all_to_all(both, "z", split_axis=0, concat_axis=0, tiled=True)
    rows = [row] + [shifted(row, "x", turn, X_CHIPS, True) for turn in range(1, X_CHIPS)]
    earlier = [shifted(part, "seq", 1, SEGMENTS, False) for part in rows]

    inner = columns % SEG_BLOCKS
    turn = (x_index - inner // ROW_BLOCKS) % X_CHIPS
    place = jnp.where(
        columns // SEG_BLOCKS == segment, turn * ROW_BLOCKS + inner % ROW_BLOCKS, -1
    )
    mine = own_columns(place.astype(jnp.int32), rows)
    chunk = (SEGMENTS, NV * 2 * BLOCK_TOKENS // SEGMENTS, HEAD_WIDTH)
    pieces = lax.all_to_all(
        mine.reshape(chunk), "seq", split_axis=0, concat_axis=0, tiled=True
    )
    piece = pieces.astype(jnp.float32).sum(0).astype(jnp.bfloat16)
    found = lax.all_to_all(
        jnp.broadcast_to(piece[None], chunk), "seq", split_axis=0, concat_axis=0, tiled=True
    ).reshape(NV, 2, BLOCK_TOKENS, HEAD_WIDTH)

    query = queries.reshape(BLOCK_TOKENS, Z_CHIPS, X_CHIPS, HEAD_WIDTH)
    query = query.transpose(2, 1, 0, 3).reshape(QUERY_HEADS, BLOCK_TOKENS, HEAD_WIDTH)
    query_here = lax.all_to_all(query, ("x", "z"), split_axis=0, concat_axis=0, tiled=True)

    index, bias, pairs = slot_tables(columns, offsets, in_use, segment, x_index)
    context = attention(index, bias, pairs, query_here, earlier + rows, found)
    back = lax.all_to_all(context, ("x", "z"), split_axis=0, concat_axis=0, tiled=True)
    back = back.reshape(X_CHIPS, Z_CHIPS, BLOCK_TOKENS, HEAD_WIDTH).transpose(2, 1, 0, 3)
    return back.reshape(1, BLOCK_TOKENS, QUERY_HEADS * HEAD_WIDTH)


def solution(mesh):
    fine = Mesh(mesh.devices.reshape(X_CHIPS, Z_CHIPS, SEGMENTS), ("x", "z", "seq"))
    spread = P("seq", ("x", "z"), None)
    return jax.shard_map(
        shards,
        mesh=fine,
        in_specs=(spread, spread, spread, P(), P(), P()),
        out_specs=spread,
        check_vma=False,
    )
```

```python
import math

import jax
import jax.numpy as jnp
from jax import lax
from jax.experimental import pallas as pl
from jax.experimental.pallas import tpu as pltpu
from jax.sharding import Mesh
from jax.sharding import PartitionSpec as P


QUERY_HEADS = 32
KEY_VALUE_HEADS = 8
HEAD_WIDTH = 128
BLOCK_TOKENS = 128
X_CHIPS = 4
Z_CHIPS = 8
SEGMENTS = 16
NV = 6
NS = 3
SLOTS = 1 + NS + NV
ROW_BLOCKS = 8
SEG_BLOCKS = 32
COLUMN_BASE = 2 * SEG_BLOCKS
POOL_BLOCKS = COLUMN_BASE + NV
GROUP = 4


def shifted(value, axis, distance, size, wrap):
    pairs = [(i, (i + distance) % size) for i in range(size) if wrap or i + distance < size]
    return lax.ppermute(value, axis, pairs)


PART_STARTS = (0, 8, 16, 20, 24)
PART_SIZES = (8, 8, 4, 4, 8)


def column_kernel(place_ref, *refs):
    parts = refs[: len(PART_SIZES)]
    out_ref, sems = refs[len(PART_SIZES) :]
    out_ref[...] = jnp.zeros_like(out_ref)
    for slot in range(NV):
        place = place_ref[slot]
        for part, low, size in zip(parts, PART_STARTS, PART_SIZES):

            @pl.when((place >= low) & (place < low + size))
            def _():
                copy = pltpu.make_async_copy(
                    part.at[place - low], out_ref.at[slot], sems.at[slot]
                )
                copy.start()
                copy.wait()


def own_columns(place, rows):
    return pl.pallas_call(
        column_kernel,
        out_shape=jax.ShapeDtypeStruct((NV, 2, BLOCK_TOKENS, HEAD_WIDTH), jnp.bfloat16),
        grid_spec=pltpu.PrefetchScalarGridSpec(
            num_scalar_prefetch=1,
            grid=(1,),
            in_specs=[pl.BlockSpec(memory_space=pl.ANY)] * len(PART_SIZES),
            out_specs=pl.BlockSpec(
                (NV, 2, BLOCK_TOKENS, HEAD_WIDTH), lambda i, place_ref: (0, 0, 0, 0)
            ),
            scratch_shapes=[pltpu.SemaphoreType.DMA((NV,))],
        ),
        name="own_columns",
    )(place, *rows)


def attention_kernel(
    index_ref, bias_ref, pairs_ref, query_ref, *rest
):
    count = 2 * len(PART_SIZES)
    parts = rest[:count]
    columns, out_ref, pool, score_ref, top_ref, total_ref, mix_ref, sems = rest[count:]
    starts = PART_STARTS + tuple(SEG_BLOCKS + start for start in PART_STARTS)
    copies = [
        pltpu.make_async_copy(part, pool.at[pl.ds(start, size)], sems.at[at])
        for at, (part, start, size) in enumerate(zip(parts, starts, PART_SIZES * 2))
    ]
    copies.append(
        pltpu.make_async_copy(columns, pool.at[pl.ds(COLUMN_BASE, NV)], sems.at[count])
    )
    for copy in copies:
        copy.start()
    for copy in copies:
        copy.wait()
    scale = math.log2(math.e) / math.sqrt(HEAD_WIDTH)
    pairs = pairs_ref[0]
    row_ids = lax.broadcasted_iota(jnp.int32, (BLOCK_TOKENS, BLOCK_TOKENS), 0)
    col_ids = lax.broadcasted_iota(jnp.int32, (BLOCK_TOKENS, BLOCK_TOKENS), 1)
    causal_bias = jnp.where(row_ids >= col_ids, 0.0, -jnp.inf)

    def keys_of(slot, block, part):
        return pool[index_ref[slot, block], part]

    def score(pair, group, first):
        for at in range(GROUP):
            block = group * GROUP + at
            key_pair = jnp.concatenate(
                [keys_of(2 * pair, block, 0), keys_of(2 * pair + 1, block, 0)], axis=0
            )
            found = lax.dot_general(
                query_ref[block],
                key_pair,
                (((1,), (1,)), ((), ())),
                preferred_element_type=jnp.float32,
            )
            left = found[:, :BLOCK_TOKENS]
            right = found[:, BLOCK_TOKENS:] + bias_ref[2 * pair + 1, block]
            if first:
                left = left + causal_bias
                top_ref[at] = jnp.maximum(left, right)
            else:
                left = left + bias_ref[2 * pair, block]
                top_ref[at] = jnp.maximum(top_ref[at], jnp.maximum(left, right))
            score_ref[pair, at, :, :BLOCK_TOKENS] = left
            score_ref[pair, at, :, BLOCK_TOKENS:] = right

    def mix(pair, group, first):
        for at in range(GROUP):
            block = group * GROUP + at
            value_pair = jnp.concatenate(
                [keys_of(2 * pair, block, 1), keys_of(2 * pair + 1, block, 1)], axis=0
            )
            top = top_ref[at]
            top = jnp.concatenate([top, top], axis=1)
            weights = jnp.exp2((score_ref[pair, at] - top) * scale)
            total = weights[:, :BLOCK_TOKENS] + weights[:, BLOCK_TOKENS:]
            mixed = jnp.dot(
                weights.astype(jnp.bfloat16), value_pair, preferred_element_type=jnp.float32
            )
            if first:
                total_ref[at] = total
                mix_ref[at] = mixed
            else:
                total_ref[at] += total
                mix_ref[at] += mixed

    def group_step(group, carry):
        score(0, group, True)

        def score_step(pair, inner):
            score(pair, group, False)
            return inner

        lax.fori_loop(1, pairs, score_step, 0)
        for at in range(GROUP):
            top_ref[at] = jnp.broadcast_to(
                jnp.max(top_ref[at], axis=1, keepdims=True), (BLOCK_TOKENS, BLOCK_TOKENS)
            )
        mix(0, group, True)

        def mix_step(pair, inner):
            mix(pair, group, False)
            return inner

        lax.fori_loop(1, pairs, mix_step, 0)
        for at in range(GROUP):
            total = jnp.sum(total_ref[at], axis=1, keepdims=True)
            out_ref[group * GROUP + at] = (mix_ref[at] / total).astype(out_ref.dtype)
        return carry

    lax.fori_loop(0, SEG_BLOCKS // GROUP, group_step, 0)


def attention(index, bias, pairs, query, rows, columns):
    whole = (SEG_BLOCKS, BLOCK_TOKENS, HEAD_WIDTH)
    square = (GROUP, BLOCK_TOKENS, BLOCK_TOKENS)
    return pl.pallas_call(
        attention_kernel,
        out_shape=jax.ShapeDtypeStruct(whole, jnp.bfloat16),
        grid_spec=pltpu.PrefetchScalarGridSpec(
            num_scalar_prefetch=3,
            grid=(1,),
            in_specs=[pl.BlockSpec(whole, lambda i, *refs: (0, 0, 0))]
            + [pl.BlockSpec(memory_space=pl.ANY)] * (2 * len(PART_SIZES) + 1),
            out_specs=pl.BlockSpec(whole, lambda i, *refs: (0, 0, 0)),
            scratch_shapes=[
                pltpu.VMEM((POOL_BLOCKS, 2, BLOCK_TOKENS, HEAD_WIDTH), jnp.bfloat16),
                pltpu.VMEM((SLOTS // 2, GROUP, BLOCK_TOKENS, 2 * BLOCK_TOKENS), jnp.float32),
                pltpu.VMEM(square, jnp.float32),
                pltpu.VMEM(square, jnp.float32),
                pltpu.VMEM(square, jnp.float32),
                pltpu.SemaphoreType.DMA((2 * len(PART_SIZES) + 1,)),
            ],
        ),
        name="attention",
    )(index, bias, pairs, query, *rows, columns)


def slot_tables(columns, offsets, in_use, segment, x_index):
    slots = jnp.arange(SLOTS, dtype=jnp.int32)
    local = jnp.arange(SEG_BLOCKS, dtype=jnp.int32)
    blocks = segment * SEG_BLOCKS + local
    live_slash = jnp.arange(NS, dtype=jnp.int32) < in_use[1]
    slash_hit = slots[:, None] - 1 == jnp.arange(NS, dtype=jnp.int32)[None, :]
    offset = jnp.sum(jnp.where(slash_hit & live_slash[None, :], offsets[None, :], 0), axis=1)
    is_slash = (slots >= 1) & (slots <= in_use[1])
    column_slot = slots - 1 - in_use[1]
    is_column = (column_slot >= 0) & (column_slot < in_use[0])
    column_hit = column_slot[:, None] == jnp.arange(NV, dtype=jnp.int32)[None, :]
    column = jnp.sum(jnp.where(column_hit, columns[None, :], 0), axis=1)
    repeated = jnp.any(
        live_slash[None, None, :]
        & (blocks[None, :, None] - column[:, None, None] == offsets[None, None, :]),
        axis=2,
    )
    column_ok = is_column[:, None] & (column[:, None] < blocks[None, :]) & ~repeated
    slash_ok = is_slash[:, None] & (blocks[None, :] >= offset[:, None])
    source = local[None, :] - offset[:, None] + SEG_BLOCKS
    own = source // SEG_BLOCKS
    inner = source % SEG_BLOCKS
    turn = (x_index - inner // ROW_BLOCKS) % X_CHIPS
    near = own * SEG_BLOCKS + turn * ROW_BLOCKS + inner % ROW_BLOCKS
    far = jnp.clip(COLUMN_BASE + column_slot, COLUMN_BASE, POOL_BLOCKS - 1)
    index = jnp.where(is_column[:, None], far[:, None], near)
    active = (slots == 0)[:, None] | slash_ok | column_ok
    bias = jnp.where(active, 0.0, -jnp.inf).astype(jnp.float32)
    pairs = (in_use[0] + in_use[1] + 2) // 2
    return index.astype(jnp.int32), bias, pairs.astype(jnp.int32).reshape(1)


def shards(queries, key_row_matrix, values, verticals, slashes, counts):
    segment = lax.axis_index("seq")
    x_index = lax.axis_index("x")
    head = lax.axis_index("z") * X_CHIPS + x_index
    columns = lax.dynamic_index_in_dim(verticals, head, 0, keepdims=False)
    offsets = lax.dynamic_index_in_dim(slashes, head, 0, keepdims=False)
    in_use = lax.dynamic_index_in_dim(counts, head, 0, keepdims=False)

    tile = (BLOCK_TOKENS, KEY_VALUE_HEADS, HEAD_WIDTH)
    both = jnp.stack(
        [key_row_matrix.reshape(tile), values.reshape(tile)], axis=0
    ).transpose(2, 0, 1, 3)
    row = lax.all_to_all(both, "z", split_axis=0, concat_axis=0, tiled=True)
    after = shifted(row, "x", 1, X_CHIPS, True)
    before = shifted(row, "x", X_CHIPS - 1, X_CHIPS, True)
    earlier0 = shifted(row, "seq", 1, SEGMENTS, False)
    half = ROW_BLOCKS // 2
    across = [
        shifted(after[:half], "x", 1, X_CHIPS, True),
        shifted(before[half:], "x", X_CHIPS - 1, X_CHIPS, True),
    ]
    earlier1 = shifted(after, "seq", 1, SEGMENTS, False)
    earlier3 = shifted(before, "seq", 1, SEGMENTS, False)
    earlier2 = [shifted(part, "seq", 1, SEGMENTS, False) for part in across]
    rows = [row, after] + across + [before]
    earlier = [earlier0, earlier1] + earlier2 + [earlier3]

    inner = columns % SEG_BLOCKS
    turn = (x_index - inner // ROW_BLOCKS) % X_CHIPS
    place = jnp.where(
        columns // SEG_BLOCKS == segment, turn * ROW_BLOCKS + inner % ROW_BLOCKS, -1
    )
    mine = own_columns(place.astype(jnp.int32), rows)
    chunk = (SEGMENTS, NV * 2 * BLOCK_TOKENS // SEGMENTS, HEAD_WIDTH)
    pieces = lax.all_to_all(
        mine.reshape(chunk), "seq", split_axis=0, concat_axis=0, tiled=True
    )
    piece = pieces.astype(jnp.float32).sum(0).astype(jnp.bfloat16)
    wide = jnp.broadcast_to(piece[None], chunk)
    found = lax.all_to_all(wide, "seq", split_axis=0, concat_axis=0, tiled=True)
    found = found.reshape(NV, 2, BLOCK_TOKENS, HEAD_WIDTH)

    query = queries.reshape(BLOCK_TOKENS, Z_CHIPS, X_CHIPS, HEAD_WIDTH)
    query = query.transpose(2, 1, 0, 3).reshape(QUERY_HEADS, BLOCK_TOKENS, HEAD_WIDTH)
    query_here = lax.all_to_all(
        query, ("x", "z"), split_axis=0, concat_axis=0, tiled=True
    )

    index, bias, pairs = slot_tables(columns, offsets, in_use, segment, x_index)
    context = attention(index, bias, pairs, query_here, earlier + rows, found)
    back = lax.all_to_all(context, ("x", "z"), split_axis=0, concat_axis=0, tiled=True)
    back = back.reshape(X_CHIPS, Z_CHIPS, BLOCK_TOKENS, HEAD_WIDTH).transpose(2, 1, 0, 3)
    return back.reshape(1, BLOCK_TOKENS, QUERY_HEADS * HEAD_WIDTH)


def solution(mesh):
    fine = Mesh(mesh.devices.reshape(X_CHIPS, Z_CHIPS, SEGMENTS), ("x", "z", "seq"))
    spread = P("seq", ("x", "z"), None)
    return jax.shard_map(
        shards,
        mesh=fine,
        in_specs=(spread, spread, spread, P(), P(), P()),
        out_specs=spread,
        check_vma=False,
    )
```

```python
import math

import jax
import jax.numpy as jnp
from jax import lax
from jax.experimental import pallas as pl
from jax.experimental.pallas import tpu as pltpu
from jax.sharding import Mesh
from jax.sharding import PartitionSpec as P


QUERY_HEADS = 32
KEY_VALUE_HEADS = 8
HEAD_WIDTH = 128
BLOCK_TOKENS = 128
X_CHIPS = 4
Z_CHIPS = 8
SEGMENTS = 16
NV = 6
NS = 3
SEG_BLOCKS = 32
GROUP = X_CHIPS
SCALE = math.log2(math.e) / math.sqrt(HEAD_WIDTH)
SQUARE = (BLOCK_TOKENS, HEAD_WIDTH)
PART_STARTS = (0, 8, 16, 20, 24)
PART_SIZES = (8, 8, 4, 4, 8)
PARTS = len(PART_SIZES)


def shifted(value, axis, distance, size, wrap):
    pairs = [(i, (i + distance) % size) for i in range(size) if wrap or i + distance < size]
    return lax.ppermute(value, axis, pairs)


def scalars(count):
    return [pl.BlockSpec(memory_space=pltpu.SMEM)] * count


def pack_kernel(key_ref, value_ref, out_ref):
    for head in range(KEY_VALUE_HEADS):
        lanes = slice(head * HEAD_WIDTH, (head + 1) * HEAD_WIDTH)
        out_ref[head, 0] = key_ref[:, lanes]
        out_ref[head, 1] = value_ref[:, lanes]


def packed(keys, values):
    return pl.pallas_call(
        pack_kernel,
        out_shape=jax.ShapeDtypeStruct((KEY_VALUE_HEADS, 2) + SQUARE, jnp.bfloat16),
        name="packed",
    )(keys, values)


def deal_kernel(place_ref, query_ref, *out_refs):
    x_index = place_ref[1]
    for turn, out_ref in enumerate(out_refs):
        column = (x_index + turn) & (X_CHIPS - 1)
        for row in range(Z_CHIPS):
            start = pl.multiple_of((row * X_CHIPS + column) * HEAD_WIDTH, HEAD_WIDTH)
            out_ref[row] = query_ref[:, pl.ds(start, HEAD_WIDTH)]


def dealt(place, query):
    whole = pl.BlockSpec(memory_space=pltpu.VMEM)
    return pl.pallas_call(
        deal_kernel,
        out_shape=[jax.ShapeDtypeStruct((Z_CHIPS,) + SQUARE, jnp.bfloat16)] * X_CHIPS,
        in_specs=scalars(1) + [whole],
        out_specs=[whole] * X_CHIPS,
        name="dealt",
    )(place, query)


def pool_index(source, x_index):
    own = source >> 5
    inner = source & (SEG_BLOCKS - 1)
    turn = (x_index - (inner >> 3)) & (X_CHIPS - 1)
    return own * SEG_BLOCKS + turn * Z_CHIPS + (inner & (Z_CHIPS - 1))


def column_kernel(place_ref, vertical_ref, *refs):
    parts = refs[:PARTS]
    out_ref, sems = refs[PARTS:]
    segment, x_index, head = place_ref[0], place_ref[1], place_ref[2]
    out_ref[...] = jnp.zeros_like(out_ref)
    for slot in range(NV):
        column = vertical_ref[head, slot]
        at = pool_index(column & (SEG_BLOCKS - 1), x_index)
        mine = (column >> 5) == segment
        for part, low, size in zip(parts, PART_STARTS, PART_SIZES):

            @pl.when(mine & (at >= low) & (at < low + size))
            def _():
                copy = pltpu.make_async_copy(
                    part.at[at - low], out_ref.at[slot], sems.at[slot]
                )
                copy.start()
                copy.wait()


def own_columns(place, verticals, parts):
    return pl.pallas_call(
        column_kernel,
        out_shape=jax.ShapeDtypeStruct((NV, 2) + SQUARE, jnp.bfloat16),
        in_specs=scalars(2) + [pl.BlockSpec(memory_space=pl.ANY)] * PARTS,
        out_specs=pl.BlockSpec(memory_space=pltpu.VMEM),
        scratch_shapes=[pltpu.SemaphoreType.DMA((NV,))],
        name="own_columns",
    )(place, verticals, *parts)


def two_blocks(pool, left, right, part):
    return jnp.concatenate([pool[left, part], pool[right, part]], axis=0)


def scores_of(query, keys):
    return lax.dot_general(
        query, keys, (((1,), (1,)), ((), ())), preferred_element_type=jnp.float32
    )


def weigh(score_ref, top_ref, pair, at):
    top = top_ref[at]
    top = jnp.concatenate([top, top], axis=1)
    weights = jnp.exp2((score_ref[pair, at] - top) * SCALE)
    total = weights[:, :BLOCK_TOKENS] + weights[:, BLOCK_TOKENS:]
    return weights.astype(jnp.bfloat16), total


def bias_of(active):
    return jnp.where(active, 0.0, -jnp.inf).astype(jnp.float32)


def wide_top(top):
    return jnp.broadcast_to(jnp.max(top, axis=1, keepdims=True), SQUARE)


def near_kernel(place_ref, slash_ref, count_ref, query_ref, *refs):
    parts = refs[: 2 * PARTS]
    mix_ref, stat_ref, pool, score_ref, top_ref, total_ref, sems = refs[2 * PARTS :]
    step = pl.program_id(0)
    segment, x_index, head = place_ref[0], place_ref[1], place_ref[2]
    used = count_ref[head, 1]
    pairs = (used + 2) >> 1

    @pl.when(step == 0)
    def _():
        starts = PART_STARTS + tuple(SEG_BLOCKS + start for start in PART_STARTS)
        copies = [
            pltpu.make_async_copy(part, pool.at[pl.ds(start, size)], sems.at[at])
            for at, (part, start, size) in enumerate(zip(parts, starts, PART_SIZES * 2))
        ]
        for copy in copies:
            copy.start()
        for copy in copies:
            copy.wait()

    blocks = [((x_index - at) & (X_CHIPS - 1)) * Z_CHIPS + step for at in range(GROUP)]
    row_ids = lax.broadcasted_iota(jnp.int32, SQUARE, 0)
    col_ids = lax.broadcasted_iota(jnp.int32, SQUARE, 1)

    def offset_of(slot):
        live = slot <= used
        return jnp.where(live, slash_ref[head, jnp.clip(slot - 1, 0, NS - 1)], 0), live

    def place_of(offset, block):
        return pool_index(block - offset + SEG_BLOCKS, x_index)

    def score(pair, first):
        offsets = [(0, True) if first else offset_of(2 * pair), offset_of(2 * pair + 1)]
        for at, block in enumerate(blocks):
            spots = [place_of(offset, block) for offset, _ in offsets]
            found = scores_of(query_ref[0, at], two_blocks(pool, *spots, 0))
            reach = segment * SEG_BLOCKS + block
            right = found[:, BLOCK_TOKENS:] + bias_of(
                offsets[1][1] & (reach >= offsets[1][0])
            )
            left = found[:, :BLOCK_TOKENS]
            if first:
                left = jnp.where(row_ids >= col_ids, left, -jnp.inf)
                top_ref[at] = jnp.maximum(left, right)
            else:
                left = left + bias_of(offsets[0][1] & (reach >= offsets[0][0]))
                top_ref[at] = jnp.maximum(top_ref[at], jnp.maximum(left, right))
            score_ref[pair, at, :, :BLOCK_TOKENS] = left
            score_ref[pair, at, :, BLOCK_TOKENS:] = right

    def mix(pair, first):
        offsets = [0 if first else offset_of(2 * pair)[0], offset_of(2 * pair + 1)[0]]
        for at, block in enumerate(blocks):
            spots = [place_of(offset, block) for offset in offsets]
            weights, total = weigh(score_ref, top_ref, pair, at)
            mixed = jnp.dot(
                weights, two_blocks(pool, *spots, 1), preferred_element_type=jnp.float32
            )
            if first:
                total_ref[at] = total
                mix_ref[0, at] = mixed
            else:
                total_ref[at] += total
                mix_ref[0, at] += mixed

    score(0, True)

    @pl.when(pairs > 1)
    def _():
        score(1, False)

    for at in range(GROUP):
        top_ref[at] = wide_top(top_ref[at])
    mix(0, True)

    @pl.when(pairs > 1)
    def _():
        mix(1, False)

    for at in range(GROUP):
        total = jnp.sum(total_ref[at], axis=1, keepdims=True)
        stat_ref[0, at] = jnp.where(
            col_ids < BLOCK_TOKENS // 2, top_ref[at], jnp.broadcast_to(total, SQUARE)
        )


def near_part(place, slashes, counts, query, parts):
    group = (1, GROUP) + SQUARE
    spec = pl.BlockSpec(group, lambda i: (i, 0, 0, 0))
    state = jax.ShapeDtypeStruct((Z_CHIPS, GROUP) + SQUARE, jnp.float32)
    return pl.pallas_call(
        near_kernel,
        out_shape=[state, state],
        grid=(Z_CHIPS,),
        in_specs=scalars(3) + [spec] + [pl.BlockSpec(memory_space=pl.ANY)] * (2 * PARTS),
        out_specs=[spec, spec],
        scratch_shapes=[
            pltpu.VMEM((2 * SEG_BLOCKS, 2) + SQUARE, jnp.bfloat16),
            pltpu.VMEM((2, GROUP, BLOCK_TOKENS, 2 * BLOCK_TOKENS), jnp.float32),
            pltpu.VMEM((GROUP,) + SQUARE, jnp.float32),
            pltpu.VMEM((GROUP,) + SQUARE, jnp.float32),
            pltpu.SemaphoreType.DMA((2 * PARTS,)),
        ],
        name="near_part",
    )(place, slashes, counts, query, *parts)


def far_kernel(
    place_ref,
    vertical_ref,
    slash_ref,
    count_ref,
    query_ref,
    mix_ref,
    stat_ref,
    pool,
    out_ref,
    score_ref,
    top_ref,
    total_ref,
    sum_ref,
):
    step = pl.program_id(0)
    segment, x_index, head = place_ref[0], place_ref[1], place_ref[2]
    used = count_ref[head, 0]
    pairs = (used + 1) >> 1
    turns = [(x_index - at) & (X_CHIPS - 1) for at in range(GROUP)]

    def active(slot, at):
        column = vertical_ref[head, slot]
        distance = segment * SEG_BLOCKS + turns[at] * Z_CHIPS + step - column
        keep = (slot < used) & (distance > 0)
        for which in range(NS):
            keep &= (which >= count_ref[head, 1]) | (distance != slash_ref[head, which])
        return bias_of(keep)

    for at in range(GROUP):
        top_ref[at] = jnp.broadcast_to(stat_ref[0, at, :, :1], SQUARE)

    def score(pair, carry):
        keys = two_blocks(pool, 2 * pair, 2 * pair + 1, 0)
        for at in range(GROUP):
            found = scores_of(query_ref[0, at], keys)
            left = found[:, :BLOCK_TOKENS] + active(2 * pair, at)
            right = found[:, BLOCK_TOKENS:] + active(2 * pair + 1, at)
            top_ref[at] = jnp.maximum(top_ref[at], jnp.maximum(left, right))
            score_ref[pair, at, :, :BLOCK_TOKENS] = left
            score_ref[pair, at, :, BLOCK_TOKENS:] = right
        return carry

    lax.fori_loop(0, pairs, score, 0)
    for at in range(GROUP):
        top = wide_top(top_ref[at])
        shrink = jnp.exp2((jnp.broadcast_to(stat_ref[0, at, :, :1], SQUARE) - top) * SCALE)
        top_ref[at] = top
        half = BLOCK_TOKENS // 2
        before = jnp.broadcast_to(stat_ref[0, at, :, half : half + 1], SQUARE)
        total_ref[at] = before * shrink * (1.0 / BLOCK_TOKENS)
        sum_ref[at] = mix_ref[0, at] * shrink

    def mix(pair, carry):
        values = two_blocks(pool, 2 * pair, 2 * pair + 1, 1)
        for at in range(GROUP):
            weights, total = weigh(score_ref, top_ref, pair, at)
            total_ref[at] += total
            sum_ref[at] += jnp.dot(weights, values, preferred_element_type=jnp.float32)
        return carry

    lax.fori_loop(0, pairs, mix, 0)
    for at in range(GROUP):
        total = jnp.sum(total_ref[at], axis=1, keepdims=True)
        out_ref[turns[at], 0] = (sum_ref[at] / total).astype(out_ref.dtype)


def far_part(place, verticals, slashes, counts, query, mixed, stats, columns):
    spec = pl.BlockSpec((1, GROUP) + SQUARE, lambda i: (i, 0, 0, 0))
    return pl.pallas_call(
        far_kernel,
        out_shape=jax.ShapeDtypeStruct((X_CHIPS, Z_CHIPS) + SQUARE, jnp.bfloat16),
        grid=(Z_CHIPS,),
        in_specs=scalars(4)
        + [spec] * 3
        + [pl.BlockSpec((NV, 2) + SQUARE, lambda i: (0, 0, 0, 0))],
        out_specs=pl.BlockSpec((X_CHIPS, 1) + SQUARE, lambda i: (0, i, 0, 0)),
        scratch_shapes=[
            pltpu.VMEM((NV // 2, GROUP, BLOCK_TOKENS, 2 * BLOCK_TOKENS), jnp.float32),
            pltpu.VMEM((GROUP,) + SQUARE, jnp.float32),
            pltpu.VMEM((GROUP,) + SQUARE, jnp.float32),
            pltpu.VMEM((GROUP,) + SQUARE, jnp.float32),
        ],
        name="far_part",
    )(place, verticals, slashes, counts, query, mixed, stats, columns)


def swapped(value, axes):
    return lax.all_to_all(value, axes, split_axis=0, concat_axis=0, tiled=True)


def shards(queries, key_row_matrix, values, verticals, slashes, counts):
    segment = lax.axis_index("seq")
    x_index = lax.axis_index("x")
    head = lax.axis_index("z") * X_CHIPS + x_index
    place = jnp.stack([segment, x_index, head]).astype(jnp.int32)

    both = packed(key_row_matrix[0], values[0])
    row = swapped(both, "z")
    hands = dealt(place, queries[0])
    hands = [hands[0]] + [
        shifted(hands[turn], "x", turn, X_CHIPS, True) for turn in range(1, X_CHIPS)
    ]
    hand = jnp.stack(hands, axis=1)
    query = swapped(hand, "z")

    after = shifted(row, "x", 1, X_CHIPS, True)
    before = shifted(row, "x", X_CHIPS - 1, X_CHIPS, True)
    earlier0 = shifted(row, "seq", 1, SEGMENTS, False)
    half = Z_CHIPS // 2
    across = [
        shifted(after[:half], "x", 1, X_CHIPS, True),
        shifted(before[half:], "x", X_CHIPS - 1, X_CHIPS, True),
    ]
    earlier1 = shifted(after, "seq", 1, SEGMENTS, False)
    earlier3 = shifted(before, "seq", 1, SEGMENTS, False)
    earlier2 = [shifted(part, "seq", 1, SEGMENTS, False) for part in across]
    rows = [row, after] + across + [before]
    earlier = [earlier0, earlier1] + earlier2 + [earlier3]

    mine = own_columns(place, verticals, rows)
    chunk = (SEGMENTS, NV * 2 * BLOCK_TOKENS // SEGMENTS, HEAD_WIDTH)
    pieces = swapped(mine.reshape(chunk), "seq")
    piece = pieces.astype(jnp.float32).sum(0).astype(jnp.bfloat16)
    wide = jnp.broadcast_to(piece[None], chunk)
    found = swapped(wide, "seq")
    found = found.reshape((NV, 2) + SQUARE)

    mixed, stats = near_part(place, slashes, counts, query, earlier + rows)
    context = far_part(place, verticals, slashes, counts, query, mixed, stats, found)
    back = swapped(context.reshape((QUERY_HEADS,) + SQUARE), ("x", "z"))
    back = back.reshape((X_CHIPS, Z_CHIPS) + SQUARE).transpose(2, 1, 0, 3)
    return back.reshape(1, BLOCK_TOKENS, QUERY_HEADS * HEAD_WIDTH)


def solution(mesh):
    fine = Mesh(mesh.devices.reshape(X_CHIPS, Z_CHIPS, SEGMENTS), ("x", "z", "seq"))
    spread = P("seq", ("x", "z"), None)
    return jax.shard_map(
        shards,
        mesh=fine,
        in_specs=(spread, spread, spread, P(), P(), P()),
        out_specs=spread,
        check_vma=False,
    )
```

```python
import math

import jax
import jax.numpy as jnp
from jax import lax
from jax.experimental import pallas as pl
from jax.experimental.pallas import tpu as pltpu
from jax.sharding import Mesh
from jax.sharding import PartitionSpec as P


QUERY_HEADS = 32
KEY_VALUE_HEADS = 8
HEAD_WIDTH = 128
BLOCK_TOKENS = 128
X_CHIPS = 4
Z_CHIPS = 8
SEGMENTS = 16
NV = 6
NS = 3
SEG_BLOCKS = 32
GROUP = 16
ROW_BLOCKS = 8
STEPS = SEG_BLOCKS // GROUP

SCALE = math.log2(math.e) / math.sqrt(HEAD_WIDTH)
SQUARE = (BLOCK_TOKENS, HEAD_WIDTH)


def shifted(value, axis, distance, size, wrap):
    pairs = [(i, (i + distance) % size) for i in range(size) if wrap or i + distance < size]
    return lax.ppermute(value, axis, pairs)


def scalars(count):
    return [pl.BlockSpec(memory_space=pltpu.SMEM)] * count


def pack_kernel(key_ref, value_ref, out_ref):
    for head in range(KEY_VALUE_HEADS):
        lanes = slice(head * HEAD_WIDTH, (head + 1) * HEAD_WIDTH)
        out_ref[head, 0] = key_ref[:, lanes]
        out_ref[head, 1] = value_ref[:, lanes]


def packed(keys, values):
    return pl.pallas_call(
        pack_kernel,
        out_shape=jax.ShapeDtypeStruct((KEY_VALUE_HEADS, 2) + SQUARE, jnp.bfloat16),
        name="packed",
    )(keys, values)


def deal_kernel(query_ref, out_ref):
    for x_index in range(X_CHIPS):
        for z_index in range(Z_CHIPS):
            start = (z_index * X_CHIPS + x_index) * HEAD_WIDTH
            out_ref[x_index * Z_CHIPS + z_index] = query_ref[:, start : start + HEAD_WIDTH]


def dealt(query):
    return pl.pallas_call(
        deal_kernel,
        out_shape=jax.ShapeDtypeStruct((QUERY_HEADS,) + SQUARE, jnp.bfloat16),
        name="dealt",
    )(query)


def pool_index(source, x_index):
    row = source >> 3
    turn = (x_index - row) & (X_CHIPS - 1)
    return ((row >> 2) * X_CHIPS + turn) * ROW_BLOCKS + (source & (ROW_BLOCKS - 1))


def column_kernel(place_ref, vertical_ref, *refs):
    rows, (out_ref, sems) = refs[:X_CHIPS], refs[X_CHIPS:]
    out_ref[...] = jnp.zeros_like(out_ref)
    for slot in range(NV):
        column = vertical_ref[place_ref[1], slot]
        at = pool_index(column & (SEG_BLOCKS - 1), place_ref[2])
        mine = (column >> 5) == place_ref[0]
        for turn, row in enumerate(rows):

            @pl.when(mine & ((at >> 3) == turn))
            def _():
                copy = pltpu.make_async_copy(
                    row.at[at & (ROW_BLOCKS - 1)], out_ref.at[slot], sems.at[slot]
                )
                copy.start()
                copy.wait()


def own_columns(place, verticals, rows):
    return pl.pallas_call(
        column_kernel,
        out_shape=jax.ShapeDtypeStruct((NV, 2) + SQUARE, jnp.bfloat16),
        in_specs=scalars(2) + [pl.BlockSpec(memory_space=pl.ANY)] * X_CHIPS,
        out_specs=pl.BlockSpec(memory_space=pltpu.VMEM),
        scratch_shapes=[pltpu.SemaphoreType.DMA((NV,))],
        name="own_columns",
    )(place, verticals, *rows)


def two_blocks(pool, left, right, part):
    return jnp.concatenate([pool[left, part], pool[right, part]], axis=0)


def scores_of(query, keys):
    return lax.dot_general(
        query, keys, (((1,), (1,)), ((), ())), preferred_element_type=jnp.float32
    )


def weigh(score_ref, top_ref, pair, at):
    top = top_ref[at]
    top = jnp.concatenate([top, top], axis=1)
    weights = jnp.exp2((score_ref[pair, at] - top) * SCALE)
    total = weights[:, :BLOCK_TOKENS] + weights[:, BLOCK_TOKENS:]
    return weights.astype(jnp.bfloat16), total


def bias_of(active):
    return jnp.where(active, 0.0, -jnp.inf).astype(jnp.float32)


def wide_top(top):
    return jnp.broadcast_to(jnp.max(top, axis=1, keepdims=True), SQUARE)


def near_kernel(
    place_ref,
    slash_ref,
    count_ref,
    query_ref,
    *refs,
):
    rows = refs[: 2 * X_CHIPS]
    mix_ref, stat_ref, pool, score_ref, top_ref, total_ref, sems = refs[2 * X_CHIPS :]
    step = pl.program_id(0)
    segment, head, x_index = place_ref[0], place_ref[1], place_ref[2]
    used = count_ref[head, 1]
    pairs = (used + 2) >> 1

    @pl.when(step == 0)
    def _():
        copies = [
            pltpu.make_async_copy(row, pool.at[pl.ds(at * ROW_BLOCKS, ROW_BLOCKS)], sems.at[at])
            for at, row in enumerate(rows)
        ]
        for copy in copies:
            copy.start()
        for copy in copies:
            copy.wait()

    blocks = [step * GROUP + at for at in range(GROUP)]
    row_ids = lax.broadcasted_iota(jnp.int32, SQUARE, 0)
    col_ids = lax.broadcasted_iota(jnp.int32, SQUARE, 1)

    def offset_of(slot):
        live = slot <= used
        return jnp.where(live, slash_ref[head, jnp.clip(slot - 1, 0, NS - 1)], 0), live

    def place_of(offset, block):
        return pool_index(block - offset + SEG_BLOCKS, x_index)

    def score(pair, first):
        offsets = [(0, True) if first else offset_of(2 * pair), offset_of(2 * pair + 1)]
        for at, block in enumerate(blocks):
            spots = [place_of(offset, block) for offset, _ in offsets]
            found = scores_of(query_ref[at], two_blocks(pool, *spots, 0))
            reach = segment * SEG_BLOCKS + block
            right = found[:, BLOCK_TOKENS:] + bias_of(
                offsets[1][1] & (reach >= offsets[1][0])
            )
            left = found[:, :BLOCK_TOKENS]
            if first:
                left = jnp.where(row_ids >= col_ids, left, -jnp.inf)
                top_ref[at] = jnp.maximum(left, right)
            else:
                left = left + bias_of(offsets[0][1] & (reach >= offsets[0][0]))
                top_ref[at] = jnp.maximum(top_ref[at], jnp.maximum(left, right))
            score_ref[pair, at, :, :BLOCK_TOKENS] = left
            score_ref[pair, at, :, BLOCK_TOKENS:] = right

    def mix(pair, first):
        offsets = [0 if first else offset_of(2 * pair)[0], offset_of(2 * pair + 1)[0]]
        for at, block in enumerate(blocks):
            spots = [place_of(offset, block) for offset in offsets]
            weights, total = weigh(score_ref, top_ref, pair, at)
            mixed = jnp.dot(
                weights, two_blocks(pool, *spots, 1), preferred_element_type=jnp.float32
            )
            if first:
                total_ref[at] = total
                mix_ref[at] = mixed
            else:
                total_ref[at] += total
                mix_ref[at] += mixed

    score(0, True)

    @pl.when(pairs > 1)
    def _():
        score(1, False)

    for at in range(GROUP):
        top_ref[at] = wide_top(top_ref[at])
    mix(0, True)

    @pl.when(pairs > 1)
    def _():
        mix(1, False)

    for at in range(GROUP):
        total = jnp.sum(total_ref[at], axis=1, keepdims=True)
        stat_ref[at] = jnp.where(
            col_ids < BLOCK_TOKENS // 2, top_ref[at], jnp.broadcast_to(total, SQUARE)
        )


def near_part(place, slashes, counts, query, rows):
    spec = pl.BlockSpec((GROUP,) + SQUARE, lambda i: (i, 0, 0))
    state = jax.ShapeDtypeStruct((SEG_BLOCKS,) + SQUARE, jnp.float32)
    return pl.pallas_call(
        near_kernel,
        out_shape=[state, state],
        grid=(STEPS,),
        in_specs=scalars(3) + [spec] + [pl.BlockSpec(memory_space=pl.ANY)] * (2 * X_CHIPS),
        out_specs=[spec, spec],
        scratch_shapes=[
            pltpu.VMEM((2 * SEG_BLOCKS, 2) + SQUARE, jnp.bfloat16),
            pltpu.VMEM((2, GROUP, BLOCK_TOKENS, 2 * BLOCK_TOKENS), jnp.float32),
            pltpu.VMEM((GROUP,) + SQUARE, jnp.float32),
            pltpu.VMEM((GROUP,) + SQUARE, jnp.float32),
            pltpu.SemaphoreType.DMA((2 * X_CHIPS,)),
        ],
        name="near_part",
    )(place, slashes, counts, query, *rows)


def far_kernel(
    place_ref,
    vertical_ref,
    slash_ref,
    count_ref,
    query_ref,
    mix_ref,
    stat_ref,
    pool,
    out_ref,
    score_ref,
    top_ref,
    total_ref,
    sum_ref,
):
    step = pl.program_id(0)
    segment, head = place_ref[0], place_ref[1]
    used = count_ref[head, 0]
    pairs = (used + 1) >> 1

    def active(slot, at):
        column = vertical_ref[head, slot]
        distance = segment * SEG_BLOCKS + step * GROUP + at - column
        keep = (slot < used) & (distance > 0)
        for which in range(NS):
            keep &= (which >= count_ref[head, 1]) | (distance != slash_ref[head, which])
        return bias_of(keep)

    for at in range(GROUP):
        top_ref[at] = jnp.broadcast_to(stat_ref[at, :, :1], SQUARE)

    def score(pair, carry):
        keys = two_blocks(pool, 2 * pair, 2 * pair + 1, 0)
        for at in range(GROUP):
            found = scores_of(query_ref[at], keys)
            left = found[:, :BLOCK_TOKENS] + active(2 * pair, at)
            right = found[:, BLOCK_TOKENS:] + active(2 * pair + 1, at)
            top_ref[at] = jnp.maximum(top_ref[at], jnp.maximum(left, right))
            score_ref[pair, at, :, :BLOCK_TOKENS] = left
            score_ref[pair, at, :, BLOCK_TOKENS:] = right
        return carry

    lax.fori_loop(0, pairs, score, 0)
    for at in range(GROUP):
        top = wide_top(top_ref[at])
        shrink = jnp.exp2((jnp.broadcast_to(stat_ref[at, :, :1], SQUARE) - top) * SCALE)
        top_ref[at] = top
        half = BLOCK_TOKENS // 2
        before = jnp.broadcast_to(stat_ref[at, :, half : half + 1], SQUARE)
        total_ref[at] = before * shrink * (1.0 / BLOCK_TOKENS)
        sum_ref[at] = mix_ref[at] * shrink

    def mix(pair, carry):
        values = two_blocks(pool, 2 * pair, 2 * pair + 1, 1)
        for at in range(GROUP):
            weights, total = weigh(score_ref, top_ref, pair, at)
            total_ref[at] += total
            sum_ref[at] += jnp.dot(weights, values, preferred_element_type=jnp.float32)
        return carry

    lax.fori_loop(0, pairs, mix, 0)
    for at in range(GROUP):
        total = jnp.sum(total_ref[at], axis=1, keepdims=True)
        out_ref[at] = (sum_ref[at] / total).astype(out_ref.dtype)


def far_part(place, verticals, slashes, counts, query, mixed, stats, columns):
    spec = pl.BlockSpec((GROUP,) + SQUARE, lambda i: (i, 0, 0))
    return pl.pallas_call(
        far_kernel,
        out_shape=jax.ShapeDtypeStruct((SEG_BLOCKS,) + SQUARE, jnp.bfloat16),
        grid=(STEPS,),
        in_specs=scalars(4)
        + [spec] * 3
        + [pl.BlockSpec((NV, 2) + SQUARE, lambda i: (0, 0, 0, 0))],
        out_specs=spec,
        scratch_shapes=[
            pltpu.VMEM((NV // 2, GROUP, BLOCK_TOKENS, 2 * BLOCK_TOKENS), jnp.float32),
            pltpu.VMEM((GROUP,) + SQUARE, jnp.float32),
            pltpu.VMEM((GROUP,) + SQUARE, jnp.float32),
            pltpu.VMEM((GROUP,) + SQUARE, jnp.float32),
        ],
        name="far_part",
    )(place, verticals, slashes, counts, query, mixed, stats, columns)


def swapped(value, axes):
    return lax.all_to_all(value, axes, split_axis=0, concat_axis=0, tiled=True)


def shards(queries, key_row_matrix, values, verticals, slashes, counts):
    segment = lax.axis_index("seq")
    x_index = lax.axis_index("x")
    head = lax.axis_index("z") * X_CHIPS + x_index
    place = jnp.stack([segment, head, x_index]).astype(jnp.int32)

    both = packed(key_row_matrix[0], values[0])
    row = swapped(both, "z")
    hand = dealt(queries[0])
    query = swapped(hand, ("x", "z"))
    rows = [row]
    for turn in (1, 2, 3):
        rows.append(shifted(row, "x", turn, X_CHIPS, True))
    earlier = []
    for turn in range(X_CHIPS):
        earlier.append(shifted(rows[turn], "seq", 1, SEGMENTS, False))

    mine = own_columns(place, verticals, rows)
    chunk = (SEGMENTS, NV * 2 * BLOCK_TOKENS // SEGMENTS, HEAD_WIDTH)
    pieces = swapped(mine.reshape(chunk), "seq")
    piece = pieces.astype(jnp.float32).sum(0).astype(jnp.bfloat16)
    wide = jnp.broadcast_to(piece[None], chunk)
    found = swapped(wide, "seq")
    found = found.reshape((NV, 2) + SQUARE)

    mixed, stats = near_part(place, slashes, counts, query, earlier + rows)
    context = far_part(place, verticals, slashes, counts, query, mixed, stats, found)
    back = swapped(context, ("x", "z"))
    back = back.reshape((X_CHIPS, Z_CHIPS) + SQUARE).transpose(2, 1, 0, 3)
    return back.reshape(1, BLOCK_TOKENS, QUERY_HEADS * HEAD_WIDTH)


def solution(mesh):
    fine = Mesh(mesh.devices.reshape(X_CHIPS, Z_CHIPS, SEGMENTS), ("x", "z", "seq"))
    spread = P("seq", ("x", "z"), None)
    return jax.shard_map(
        shards,
        mesh=fine,
        in_specs=(spread, spread, spread, P(), P(), P()),
        out_specs=spread,
        check_vma=False,
    )
```

```python
import math

import jax
import jax.numpy as jnp
from jax import lax
from jax.experimental import pallas as pl
from jax.experimental.pallas import tpu as pltpu
from jax.sharding import Mesh
from jax.sharding import PartitionSpec as P


QUERY_HEADS = 32
KEY_VALUE_HEADS = 8
HEAD_WIDTH = 128
BLOCK_TOKENS = 128
X_CHIPS = 4
Z_CHIPS = 8
SEGMENTS = 16
NV = 6
NS = 3
SEG_BLOCKS = 32
GROUP = 32
ROW_BLOCKS = 8
PART_STARTS = (0, 8, 16, 20, 24)
PART_SIZES = (8, 8, 4, 4, 8)
PARTS = len(PART_SIZES)
STEPS = SEG_BLOCKS // GROUP

SCALE = math.log2(math.e) / math.sqrt(HEAD_WIDTH)
SQUARE = (BLOCK_TOKENS, HEAD_WIDTH)


def shifted(value, axis, distance, size, wrap):
    pairs = [(i, (i + distance) % size) for i in range(size) if wrap or i + distance < size]
    return lax.ppermute(value, axis, pairs)


def scalars(count):
    return [pl.BlockSpec(memory_space=pltpu.SMEM)] * count


def pack_kernel(key_ref, value_ref, out_ref):
    for head in range(KEY_VALUE_HEADS):
        lanes = slice(head * HEAD_WIDTH, (head + 1) * HEAD_WIDTH)
        out_ref[head, 0] = key_ref[:, lanes]
        out_ref[head, 1] = value_ref[:, lanes]


def packed(keys, values):
    return pl.pallas_call(
        pack_kernel,
        out_shape=jax.ShapeDtypeStruct((KEY_VALUE_HEADS, 2) + SQUARE, jnp.bfloat16),
        name="packed",
    )(keys, values)


def deal_kernel(query_ref, out_ref):
    for x_index in range(X_CHIPS):
        for z_index in range(Z_CHIPS):
            start = (z_index * X_CHIPS + x_index) * HEAD_WIDTH
            out_ref[x_index * Z_CHIPS + z_index] = query_ref[:, start : start + HEAD_WIDTH]


def dealt(query):
    return pl.pallas_call(
        deal_kernel,
        out_shape=jax.ShapeDtypeStruct((QUERY_HEADS,) + SQUARE, jnp.bfloat16),
        name="dealt",
    )(query)


def return_kernel(back_ref, out_ref):
    for x_index in range(X_CHIPS):
        for z_index in range(Z_CHIPS):
            start = (z_index * X_CHIPS + x_index) * HEAD_WIDTH
            out_ref[:, start : start + HEAD_WIDTH] = back_ref[x_index * Z_CHIPS + z_index]


def returned(back):
    return pl.pallas_call(
        return_kernel,
        out_shape=jax.ShapeDtypeStruct((BLOCK_TOKENS, QUERY_HEADS * HEAD_WIDTH), jnp.bfloat16),
        name="returned",
    )(back)


def join_kernel(pieces_ref, out_ref):
    total = pieces_ref[0].astype(jnp.float32)
    for at in range(1, SEGMENTS):
        total += pieces_ref[at].astype(jnp.float32)
    total = total.astype(jnp.bfloat16)
    for at in range(SEGMENTS):
        out_ref[at] = total


def joined(pieces):
    return pl.pallas_call(
        join_kernel,
        out_shape=jax.ShapeDtypeStruct(pieces.shape, jnp.bfloat16),
        in_specs=[pl.BlockSpec(memory_space=pltpu.VMEM)],
        out_specs=pl.BlockSpec(memory_space=pltpu.VMEM),
        name="joined",
    )(pieces)


def pool_index(source, x_index):
    row = source >> 3
    turn = (x_index - row) & (X_CHIPS - 1)
    return ((row >> 2) * X_CHIPS + turn) * ROW_BLOCKS + (source & (ROW_BLOCKS - 1))


def column_kernel(place_ref, vertical_ref, *refs):
    parts, (out_ref, sems) = refs[:PARTS], refs[PARTS:]
    out_ref[...] = jnp.zeros_like(out_ref)
    for slot in range(NV):
        column = vertical_ref[place_ref[1], slot]
        at = pool_index(column & (SEG_BLOCKS - 1), place_ref[2])
        mine = (column >> 5) == place_ref[0]
        for part, low, size in zip(parts, PART_STARTS, PART_SIZES):

            @pl.when(mine & (at >= low) & (at < low + size))
            def _():
                copy = pltpu.make_async_copy(
                    part.at[at - low], out_ref.at[slot], sems.at[slot]
                )
                copy.start()
                copy.wait()


def own_columns(place, verticals, rows):
    return pl.pallas_call(
        column_kernel,
        out_shape=jax.ShapeDtypeStruct((NV, 2) + SQUARE, jnp.bfloat16),
        in_specs=scalars(2) + [pl.BlockSpec(memory_space=pl.ANY)] * PARTS,
        out_specs=pl.BlockSpec(memory_space=pltpu.VMEM),
        scratch_shapes=[pltpu.SemaphoreType.DMA((NV,))],
        name="own_columns",
    )(place, verticals, *rows)


def two_blocks(pool, left, right, part):
    return jnp.concatenate([pool[left, part], pool[right, part]], axis=0)


def scores_of(query, keys):
    return lax.dot_general(
        query, keys, (((1,), (1,)), ((), ())), preferred_element_type=jnp.float32
    )


def weigh(score_ref, top_ref, pair, at):
    top = top_ref[at]
    top = jnp.concatenate([top, top], axis=1)
    weights = jnp.exp2((score_ref[pair, at] - top) * SCALE)
    total = weights[:, :BLOCK_TOKENS] + weights[:, BLOCK_TOKENS:]
    return weights.astype(jnp.bfloat16), total


def bias_of(active):
    return jnp.where(active, 0.0, -jnp.inf).astype(jnp.float32)


def wide_top(top):
    return jnp.broadcast_to(jnp.max(top, axis=1, keepdims=True), SQUARE)


def near_kernel(
    place_ref,
    slash_ref,
    count_ref,
    query_ref,
    *refs,
):
    parts = refs[: 2 * PARTS]
    mix_ref, stat_ref, pool, score_ref, top_ref, total_ref, sems = refs[2 * PARTS :]
    step = pl.program_id(0)
    segment, head, x_index = place_ref[0], place_ref[1], place_ref[2]
    used = count_ref[head, 1]
    pairs = (used + 2) >> 1

    @pl.when(step == 0)
    def _():
        starts = PART_STARTS + tuple(SEG_BLOCKS + start for start in PART_STARTS)
        copies = [
            pltpu.make_async_copy(part, pool.at[pl.ds(start, size)], sems.at[at])
            for at, (part, start, size) in enumerate(zip(parts, starts, PART_SIZES * 2))
        ]
        for copy in copies:
            copy.start()
        for copy in copies:
            copy.wait()

    blocks = [step * GROUP + at for at in range(GROUP)]
    row_ids = lax.broadcasted_iota(jnp.int32, SQUARE, 0)
    col_ids = lax.broadcasted_iota(jnp.int32, SQUARE, 1)

    def offset_of(slot):
        live = slot <= used
        return jnp.where(live, slash_ref[head, jnp.clip(slot - 1, 0, NS - 1)], 0), live

    def place_of(offset, block):
        return pool_index(block - offset + SEG_BLOCKS, x_index)

    def score(pair, first):
        offsets = [(0, True) if first else offset_of(2 * pair), offset_of(2 * pair + 1)]
        for at, block in enumerate(blocks):
            spots = [place_of(offset, block) for offset, _ in offsets]
            found = scores_of(query_ref[at], two_blocks(pool, *spots, 0))
            reach = segment * SEG_BLOCKS + block
            right = found[:, BLOCK_TOKENS:] + bias_of(
                offsets[1][1] & (reach >= offsets[1][0])
            )
            left = found[:, :BLOCK_TOKENS]
            if first:
                left = jnp.where(row_ids >= col_ids, left, -jnp.inf)
                top_ref[at] = jnp.maximum(left, right)
            else:
                left = left + bias_of(offsets[0][1] & (reach >= offsets[0][0]))
                top_ref[at] = jnp.maximum(top_ref[at], jnp.maximum(left, right))
            score_ref[pair, at, :, :BLOCK_TOKENS] = left
            score_ref[pair, at, :, BLOCK_TOKENS:] = right

    def mix(pair, first):
        offsets = [0 if first else offset_of(2 * pair)[0], offset_of(2 * pair + 1)[0]]
        for at, block in enumerate(blocks):
            spots = [place_of(offset, block) for offset in offsets]
            weights, total = weigh(score_ref, top_ref, pair, at)
            mixed = jnp.dot(
                weights, two_blocks(pool, *spots, 1), preferred_element_type=jnp.float32
            )
            if first:
                total_ref[at] = total
                mix_ref[at] = mixed
            else:
                total_ref[at] += total
                mix_ref[at] += mixed

    score(0, True)

    @pl.when(pairs > 1)
    def _():
        score(1, False)

    for at in range(GROUP):
        top_ref[at] = wide_top(top_ref[at])
    mix(0, True)

    @pl.when(pairs > 1)
    def _():
        mix(1, False)

    for at in range(GROUP):
        total = jnp.sum(total_ref[at], axis=1, keepdims=True)
        stat_ref[at] = jnp.where(
            col_ids < BLOCK_TOKENS // 2, top_ref[at], jnp.broadcast_to(total, SQUARE)
        )


def near_part(place, slashes, counts, query, rows):
    spec = pl.BlockSpec((GROUP,) + SQUARE, lambda i: (i, 0, 0))
    state = jax.ShapeDtypeStruct((SEG_BLOCKS,) + SQUARE, jnp.float32)
    return pl.pallas_call(
        near_kernel,
        out_shape=[state, state],
        grid=(STEPS,),
        in_specs=scalars(3) + [spec] + [pl.BlockSpec(memory_space=pl.ANY)] * (2 * PARTS),
        out_specs=[spec, spec],
        scratch_shapes=[
            pltpu.VMEM((2 * SEG_BLOCKS, 2) + SQUARE, jnp.bfloat16),
            pltpu.VMEM((2, GROUP, BLOCK_TOKENS, 2 * BLOCK_TOKENS), jnp.float32),
            pltpu.VMEM((GROUP,) + SQUARE, jnp.float32),
            pltpu.VMEM((GROUP,) + SQUARE, jnp.float32),
            pltpu.SemaphoreType.DMA((2 * PARTS,)),
        ],
        name="near_part",
    )(place, slashes, counts, query, *rows)


def far_kernel(
    place_ref,
    vertical_ref,
    slash_ref,
    count_ref,
    query_ref,
    mix_ref,
    stat_ref,
    pool,
    out_ref,
    score_ref,
    top_ref,
    total_ref,
    sum_ref,
):
    step = pl.program_id(0)
    segment, head = place_ref[0], place_ref[1]
    used = count_ref[head, 0]
    pairs = (used + 1) >> 1

    def active(slot, at):
        column = vertical_ref[head, slot]
        distance = segment * SEG_BLOCKS + step * GROUP + at - column
        keep = (slot < used) & (distance > 0)
        for which in range(NS):
            keep &= (which >= count_ref[head, 1]) | (distance != slash_ref[head, which])
        return bias_of(keep)

    for at in range(GROUP):
        top_ref[at] = jnp.broadcast_to(stat_ref[at, :, :1], SQUARE)

    def score(pair, carry):
        keys = two_blocks(pool, 2 * pair, 2 * pair + 1, 0)
        for at in range(GROUP):
            found = scores_of(query_ref[at], keys)
            left = found[:, :BLOCK_TOKENS] + active(2 * pair, at)
            right = found[:, BLOCK_TOKENS:] + active(2 * pair + 1, at)
            top_ref[at] = jnp.maximum(top_ref[at], jnp.maximum(left, right))
            score_ref[pair, at, :, :BLOCK_TOKENS] = left
            score_ref[pair, at, :, BLOCK_TOKENS:] = right
        return carry

    lax.fori_loop(0, pairs, score, 0)
    for at in range(GROUP):
        top = wide_top(top_ref[at])
        shrink = jnp.exp2((jnp.broadcast_to(stat_ref[at, :, :1], SQUARE) - top) * SCALE)
        top_ref[at] = top
        half = BLOCK_TOKENS // 2
        before = jnp.broadcast_to(stat_ref[at, :, half : half + 1], SQUARE)
        total_ref[at] = before * shrink * (1.0 / BLOCK_TOKENS)
        sum_ref[at] = mix_ref[at] * shrink

    def mix(pair, carry):
        values = two_blocks(pool, 2 * pair, 2 * pair + 1, 1)
        for at in range(GROUP):
            weights, total = weigh(score_ref, top_ref, pair, at)
            total_ref[at] += total
            sum_ref[at] += jnp.dot(weights, values, preferred_element_type=jnp.float32)
        return carry

    lax.fori_loop(0, pairs, mix, 0)
    for at in range(GROUP):
        total = jnp.sum(total_ref[at], axis=1, keepdims=True)
        out_ref[at] = (sum_ref[at] / total).astype(out_ref.dtype)


def far_part(place, verticals, slashes, counts, query, mixed, stats, columns):
    spec = pl.BlockSpec((GROUP,) + SQUARE, lambda i: (i, 0, 0))
    return pl.pallas_call(
        far_kernel,
        out_shape=jax.ShapeDtypeStruct((SEG_BLOCKS,) + SQUARE, jnp.bfloat16),
        grid=(STEPS,),
        in_specs=scalars(4)
        + [spec] * 3
        + [pl.BlockSpec((NV, 2) + SQUARE, lambda i: (0, 0, 0, 0))],
        out_specs=spec,
        scratch_shapes=[
            pltpu.VMEM((NV // 2, GROUP, BLOCK_TOKENS, 2 * BLOCK_TOKENS), jnp.float32),
            pltpu.VMEM((GROUP,) + SQUARE, jnp.float32),
            pltpu.VMEM((GROUP,) + SQUARE, jnp.float32),
            pltpu.VMEM((GROUP,) + SQUARE, jnp.float32),
        ],
        name="far_part",
    )(place, verticals, slashes, counts, query, mixed, stats, columns)


def swapped(value, axes):
    return lax.all_to_all(value, axes, split_axis=0, concat_axis=0, tiled=True)


def shards(queries, key_row_matrix, values, verticals, slashes, counts):
    segment = lax.axis_index("seq")
    x_index = lax.axis_index("x")
    head = lax.axis_index("z") * X_CHIPS + x_index
    place = jnp.stack([segment, head, x_index]).astype(jnp.int32)

    both = packed(key_row_matrix[0], values[0])
    row = swapped(both, "z")
    hand = dealt(queries[0])
    query = swapped(hand, ("x", "z"))
    half = ROW_BLOCKS // 2
    after = shifted(row, "x", 1, X_CHIPS, True)
    before = shifted(row, "x", X_CHIPS - 1, X_CHIPS, True)
    across = [
        shifted(after[:half], "x", 1, X_CHIPS, True),
        shifted(before[half:], "x", X_CHIPS - 1, X_CHIPS, True),
    ]
    earlier0 = shifted(row, "seq", 1, SEGMENTS, False)
    earlier1 = shifted(after, "seq", 1, SEGMENTS, False)
    earlier3 = shifted(before, "seq", 1, SEGMENTS, False)
    earlier2 = [shifted(part, "seq", 1, SEGMENTS, False) for part in across]
    rows = [row, after] + across + [before]
    earlier = [earlier0, earlier1] + earlier2 + [earlier3]

    mine = own_columns(place, verticals, rows)
    chunk = (SEGMENTS, NV * 2 * BLOCK_TOKENS // SEGMENTS, HEAD_WIDTH)
    pieces = swapped(mine.reshape(chunk), "seq")
    found = swapped(joined(pieces), "seq")
    found = found.reshape((NV, 2) + SQUARE)

    mixed, stats = near_part(place, slashes, counts, query, earlier + rows)
    context = far_part(place, verticals, slashes, counts, query, mixed, stats, found)
    back = swapped(context, ("x", "z"))
    return returned(back)[None]


def solution(mesh):
    fine = Mesh(mesh.devices.reshape(X_CHIPS, Z_CHIPS, SEGMENTS), ("x", "z", "seq"))
    spread = P("seq", ("x", "z"), None)
    return jax.shard_map(
        shards,
        mesh=fine,
        in_specs=(spread, spread, spread, P(), P(), P()),
        out_specs=spread,
        check_vma=False,
    )
```
